128 devices in a mesh: stretch: 32 (over z, y, core), section: 4 (over x).
Axes of the slice: x: 4, y: 4, z: 4, core: 2. Of those that a mesh axis runs over, the one named last changes fastest.
Arguments:
- hidden: bfloat16 [4, 16384, 4096], P('section', 'stretch'), may hold values from -64 to 64
- norm_gain: float32 [4, 4096], P('section'), may hold values from 0.5 to 1.5
- queries: bfloat16 [4, 16384, 2048], P('section', 'stretch'), may hold values from -110 to 110
- cache: bfloat16 [4, 512, 32, 4096], P('section', 'stretch'), may hold values from -35 to 35
- nbr_shard: int32 [256, 2], P('stretch'), may hold values from 0 to 31, as said below
- nbr_slot: int32 [256, 2], P('stretch'), may hold values from 0 to 15
- grad_heads: bfloat16 [4, 16384, 2048], P('section', 'stretch'), may hold values from -24 to 24
- grad_out: bfloat16 [4, 16384, 4096], P('section', 'stretch'), may hold values from -3 to 3
- query_weight: bfloat16 [4, 4096, 2048], P('section', 'stretch'), may hold values from -0.09375 to 0.09375
Outputs:
- section_grads: bfloat16 [4, 16384, 4096], P('section', 'stretch')
The draws below stay inside these ranges and needn't reach their ends.
Inputs may be any that keep to these rules, and one draw needn't show every extreme that they name: `nbr_shard`: the 2 shards of a stretch differ. In the 8 stretches of one device (aligned blocks of rows) no shard is named more than 1 times; one shard is named exactly 1 times in every such block.
All inputs are finite; a program needn't handle non-finite values.
Results may differ from the reference program's by a relative error of at most 0.0067.
Values may be sent and summed in bfloat16 or wider, within the bound.
No kernel may reach another device: no remote copies, remote signals or barrier semaphores. Data moves between devices by JAX's collectives and lax.ppermute only.
A program may use at most 192 MiB of HBM per device.

```python
import math
import jax
import jax.numpy as jnp
from jax import lax

D = 4096
HEADS = 16
HEAD_DIM = 128
STRETCH = 64
NBRS = 2
NBR_LEN = 32
CH_DEV = 8
DB_DEV = 16
QW = 2048
SHARDS = 32
CAP = 1
LAYERS = 4
STRETCHES = 256
TOKENS = 16384
DB_ROWS = 512


def draw_hidden(key, part):
    row_key, col_key, noise_key = jax.random.split(key, 3)
    row_scale = jnp.exp(jax.random.uniform(row_key, (LAYERS, TOKENS, 1), minval=math.log(0.3), maxval=math.log(3.0)))
    col_scale = jnp.exp(jax.random.uniform(col_key, (1, 1, D), minval=math.log(0.3), maxval=math.log(3.0)))
    base_noise = jax.random.normal(noise_key, (LAYERS, TOKENS, D))
    return (base_noise * row_scale * col_scale).astype(jnp.bfloat16)


def draw_queries(key, part):
    base_noise = jax.random.normal(key, (LAYERS, TOKENS, QW))
    return base_noise.astype(jnp.bfloat16)


def draw_cache(key, part):
    noise_key = jax.random.fold_in(key, 0)
    base_noise = jax.random.normal(noise_key, (LAYERS, DB_ROWS, NBR_LEN, 2 * QW))
    return base_noise.astype(jnp.bfloat16)


def draw_nbr_shard(key, part):
    hot_shard = jax.random.randint(jax.random.fold_in(key, 11), (), 0, SHARDS)
    request_count = NBRS * CH_DEV

    def one_block(block_key):
        perm_key, roll_key = jax.random.split(block_key)
        shuffled = jax.random.permutation(perm_key, SHARDS - 1).astype(jnp.int32)
        others = shuffled + (shuffled >= hot_shard).astype(jnp.int32)
        seq_pos = jnp.arange(request_count)
        group_idx = jnp.minimum(jnp.maximum(seq_pos - CAP, 0) // CAP, SHARDS - 2)
        owners = jnp.where(seq_pos < CAP, hot_shard, others[group_idx])
        offset = jax.random.randint(roll_key, (), 0, request_count)
        owners = jnp.roll(owners, offset)
        return owners.reshape(NBRS, CH_DEV).T
    block_keys = jax.random.split(jax.random.fold_in(key, 12), STRETCHES // CH_DEV)
    return jax.vmap(one_block)(block_keys).reshape(STRETCHES, NBRS).astype(jnp.int32)


def place_ends(values, key, smallest, largest):
    longest = values.shape.index(max(values.shape))
    spots = []
    for shift in (0, 1):
        where = [jax.random.randint(jax.random.fold_in(key, axis), (), 0, length) for axis, length in enumerate(values.shape)]
        where[longest] = (where[longest] + shift) % values.shape[longest]
        spots.append(tuple(where))
    return values.at[spots[0]].set(smallest).at[spots[1]].set(largest)


def shard_levels(own_key, shape, pieces, smallest, largest):
    loudness, own = 1.0, jax.random.fold_in(own_key, 6)
    for dim, shards_of in pieces:
        draws = jnp.exp(jax.random.uniform(jax.random.fold_in(own, dim), (shards_of,), jnp.float32, smallest / len(pieces), largest / len(pieces)))
        loudness = loudness * jnp.repeat(draws, shape[dim] // shards_of).reshape([-1 if axis == dim else 1 for axis in range(len(shape))])
    return loudness


def scatter_about(own_key, shape, scale, reach, pieces=(), kind=jnp.bfloat16):
    level = shard_levels(own_key, shape, pieces, -0.22, 0.18) if pieces else 1.0
    array = jax.random.normal(own_key, shape, jnp.float32) * scale * level
    return jnp.minimum(jnp.maximum(array, -reach), reach).astype(kind)


def setup_inputs(seed: int = 0) -> dict:
    key_list = jax.random.split(jax.random.key(seed), 10)
    hidden = draw_hidden(jax.random.fold_in(key_list[9], 71), 0)
    norm_gain = jnp.clip(0.5 + 1.0 * jax.random.uniform(key_list[1], (LAYERS, D), jnp.float32) ** shard_levels(key_list[1], (LAYERS, D), ((0, 4),), -0.2, 0.2), 0.5, 1.5)
    queries = draw_queries(jax.random.fold_in(key_list[9], 71), 0)
    cache = draw_cache(jax.random.fold_in(key_list[9], 71), 0)
    nbr_shard = draw_nbr_shard(jax.random.fold_in(key_list[9], 71), 0)
    nbr_slot = place_ends(jax.random.randint(key_list[5], (STRETCHES, NBRS), 0, DB_DEV), jax.random.fold_in(key_list[5], 1), 0, DB_DEV - 1).astype(jnp.int32)
    grad_heads = scatter_about(key_list[6], (LAYERS, TOKENS, QW), 4.0, 24.0, ((0, 4), (1, 32)))
    grad_out = scatter_about(key_list[7], (LAYERS, TOKENS, D), 0.5, 3.0, ((0, 4), (1, 32)))
    query_weight = scatter_about(key_list[8], (LAYERS, D, QW), D ** -0.5, 0.09375, ((0, 4), (1, 32)))
    return {"hidden": hidden, "norm_gain": norm_gain, "queries": queries, "cache": cache, "nbr_shard": nbr_shard, "nbr_slot": nbr_slot, "grad_heads": grad_heads, "grad_out": grad_out, "query_weight": query_weight}


norm_eps = 1e-05

def layer_grad(hidden, gain, queries, cache, rows, head_grads, out_grad, weight):
    factor = HEAD_DIM ** (-0.5)
    fetched = cache[rows].reshape(STRETCHES, NBRS * NBR_LEN, 2 * QW)
    key_heads = fetched[:, :, :QW].reshape(STRETCHES, NBRS * NBR_LEN, HEADS, HEAD_DIM).astype(jnp.float32)
    value_heads = fetched[:, :, QW:].reshape(STRETCHES, NBRS * NBR_LEN, HEADS, HEAD_DIM).astype(jnp.float32)
    query_heads = queries.reshape(STRETCHES, STRETCH, HEADS, HEAD_DIM).astype(jnp.float32)
    grad_split = head_grads.reshape(STRETCHES, STRETCH, HEADS, HEAD_DIM).astype(jnp.float32)
    scores = jnp.einsum('cqhd,ckhd->chqk', query_heads, key_heads) * factor
    row_max = lax.optimization_barrier(jnp.max(scores, axis=-1, keepdims=True))
    exp_scores = jnp.exp(scores - row_max)
    attn_probs = exp_scores / lax.optimization_barrier(jnp.sum(exp_scores, axis=-1, keepdims=True))
    dprob = jnp.einsum('cqhd,ckhd->chqk', grad_split, value_heads)
    row_inner = lax.optimization_barrier(jnp.sum(attn_probs * dprob, axis=-1, keepdims=True))
    dscore = (factor * attn_probs * (dprob - row_inner)).astype(jnp.bfloat16)
    query_grad = jnp.einsum('chqk,ckhd->cqhd', dscore.astype(jnp.float32), key_heads)
    query_grad = query_grad.astype(jnp.bfloat16).reshape(TOKENS, QW)
    norm_grad = jnp.dot(query_grad, weight.T, preferred_element_type=jnp.float32)
    values_in = hidden.astype(jnp.float32)
    inv_rms = lax.rsqrt(lax.optimization_barrier(jnp.mean(values_in * values_in, axis=-1, keepdims=True)) + norm_eps)
    normed = values_in * inv_rms
    scaled_grad = norm_grad * gain[None, :]
    mean_term = lax.optimization_barrier(jnp.mean(scaled_grad * normed, axis=-1, keepdims=True))
    return out_grad.astype(jnp.float32) + inv_rms * (scaled_grad - normed * mean_term)

def reference(hidden, norm_gain, queries, cache, nbr_shard, nbr_slot, grad_heads, grad_out, query_weight):
    rows = (nbr_shard * DB_DEV + nbr_slot).astype(jnp.int32)
    results = []
    for layer in range(LAYERS):
        results.append(layer_grad(hidden[layer], norm_gain[layer], queries[layer], cache[layer], rows, grad_heads[layer], grad_out[layer], query_weight[layer]))
    stacked = jnp.stack(results, axis=0)
    return jnp.roll(stacked, -1, axis=0).astype(jnp.bfloat16)
```

```python
import functools

import jax
import jax.numpy as jnp
from jax import lax
from jax.experimental import pallas as pl
from jax.experimental.pallas import tpu as pltpu
from jax.sharding import PartitionSpec as P

HEAD_DIM = 128
STRETCH = 64
norm_eps = 1e-05
CHUNKS = (8, 4, 4)
DIRECT_ROWS = 192
COLUMNS = 512


def passed_along(value, axis, steps):
    count = lax.axis_size(axis)
    pairs = [(source, (source + steps) % count) for source in range(count)]
    return lax.ppermute(value, axis, pairs)


def pick_kernel(key_at, value_at, width, picks, table, out, sem):
    for place in range(out.shape[0]):
        row = picks[place]
        pltpu.make_async_copy(
            table.at[row, :, pl.ds(key_at, width)], out.at[place, :, pl.ds(0, width)], sem
        ).start()
        pltpu.make_async_copy(
            table.at[row, :, pl.ds(value_at, width)], out.at[place, :, pl.ds(width, width)], sem
        ).start()
    pltpu.make_async_copy(out, out, sem).wait()


def picked_rows(picks, table, first, width, qwidth):
    places = picks.shape[0]
    span = table.shape[1]
    size = places * span * 2 * width
    return pl.pallas_call(
        functools.partial(pick_kernel, first, qwidth + first, width),
        out_shape=jax.ShapeDtypeStruct((places, span, 2 * width), table.dtype),
        grid_spec=pltpu.PrefetchScalarGridSpec(
            num_scalar_prefetch=1,
            grid=(1,),
            in_specs=[pl.BlockSpec(memory_space=pl.ANY)],
            out_specs=pl.BlockSpec(memory_space=pl.ANY),
            scratch_shapes=[pltpu.SemaphoreType.DMA],
        ),
        cost_estimate=pl.CostEstimate(flops=0, transcendentals=0, bytes_accessed=4 * size),
        name="pick_rows",
    )(picks, table)


def attention_kernel(heads, owners, first, second, query, grad, out):
    factor = HEAD_DIM ** (-0.5)
    width = heads * HEAD_DIM
    for head in range(heads):
        cols = slice(head * HEAD_DIM, (head + 1) * HEAD_DIM)
        vcols = slice(width + head * HEAD_DIM, width + (head + 1) * HEAD_DIM)
        keys = jnp.concatenate([first[0, :, cols], second[0, :, cols]], axis=0)
        values = jnp.concatenate([first[0, :, vcols], second[0, :, vcols]], axis=0)
        across = (((1,), (1,)), ((), ()))
        scores = (
            lax.dot_general(query[:, cols], keys, across, preferred_element_type=jnp.float32)
            * factor
        )
        dprob = lax.dot_general(
            grad[:, cols], values, across, preferred_element_type=jnp.float32
        )
        exp_scores = jnp.exp(scores - jnp.max(scores, axis=-1, keepdims=True))
        probs = exp_scores / jnp.sum(exp_scores, axis=-1, keepdims=True)
        inner = jnp.sum(probs * dprob, axis=-1, keepdims=True)
        dscore = (factor * probs * (dprob - inner)).astype(jnp.bfloat16)
        out[:, cols] = jnp.dot(dscore, keys, preferred_element_type=jnp.float32).astype(
            jnp.bfloat16
        )


def query_gradient(owners, fetched, queries, grads, first, heads):
    width = heads * HEAD_DIM
    tokens = queries.shape[0]
    stretches = tokens // STRETCH
    span = fetched.shape[1]
    block = first // width
    return pl.pallas_call(
        functools.partial(attention_kernel, heads),
        out_shape=jax.ShapeDtypeStruct((tokens, width), jnp.bfloat16),
        grid_spec=pltpu.PrefetchScalarGridSpec(
            num_scalar_prefetch=1,
            grid=(stretches,),
            in_specs=[
                pl.BlockSpec((1, span, 2 * width), lambda c, own: (own[2 * c], 0, 0)),
                pl.BlockSpec((1, span, 2 * width), lambda c, own: (own[2 * c + 1], 0, 0)),
                pl.BlockSpec((STRETCH, width), lambda c, own: (c, block)),
                pl.BlockSpec((STRETCH, width), lambda c, own: (c, block)),
            ],
            out_specs=pl.BlockSpec((STRETCH, width), lambda c, own: (c, 0)),
        ),
        cost_estimate=pl.CostEstimate(
            flops=6 * tokens * STRETCH * width,
            transcendentals=tokens * STRETCH * heads,
            bytes_accessed=2 * (3 * tokens * width + 2 * stretches * span * 2 * width),
        ),
        name="query_gradient",
    )(owners, fetched, fetched, queries, grads)


def finish_kernel(widths, near, blocks, *refs):
    parts = refs[: len(widths)]
    weight, gain, hidden_near, hidden_far, grad_out, out, scaled, dots, squares = refs[len(widths) :]
    phase, block = pl.program_id(0), pl.program_id(1)
    model = blocks * COLUMNS

    @pl.when(phase == 0)
    def _():
        total = None
        start = 0
        for part, width in zip(parts, widths):
            product = lax.dot_general(
                part[...],
                weight[:, start : start + width],
                (((1,), (1,)), ((), ())),
                preferred_element_type=jnp.float32,
            )
            total = product if total is None else total + product
            start += width
        grad = total * gain[...]
        scaled[block] = grad
        for ref, rows in ((hidden_near, slice(0, near)), (hidden_far, slice(near, None))):
            values = ref[...].astype(jnp.float32)
            cross = grad[rows] * values
            square = values * values
            dot = cross[:, :128]
            norm = square[:, :128]
            for lane in range(128, COLUMNS, 128):
                dot = dot + cross[:, lane : lane + 128]
                norm = norm + square[:, lane : lane + 128]
            size = values.shape[0]
            at = pl.ds(rows.start, size)

            @pl.when(block == 0)
            def _():
                dots[at, :] = dot
                squares[at, :] = norm

            @pl.when(block > 0)
            def _():
                dots[at, :] += dot
                squares[at, :] += norm

    @pl.when((phase == 1) & (block == 0))
    def _():
        inv = lax.rsqrt(jnp.sum(squares[...], axis=-1, keepdims=True) / model + norm_eps)
        mean = inv * jnp.sum(dots[...], axis=-1, keepdims=True) / model
        squares[...] = jnp.broadcast_to(inv, squares.shape)
        dots[...] = jnp.broadcast_to(inv * inv * mean, dots.shape)

    @pl.when(phase == 1)
    def _():
        grad = scaled[block]
        for ref, rows in ((hidden_near, slice(0, near)), (hidden_far, slice(near, None))):
            size = ref.shape[0]
            at = pl.ds(rows.start, size)
            inv = squares[at, :1]
            pull = dots[at, :1]
            out[at, :] = (
                grad_out[at, :].astype(jnp.float32)
                + inv * grad[rows]
                - pull * ref[...].astype(jnp.float32)
            ).astype(out.dtype)


def finished(parts, weight, gain, hidden_near, hidden_far, grad_out):
    tokens, model = grad_out.shape
    near, far = hidden_near.shape[0], hidden_far.shape[0]
    widths = tuple(part.shape[1] for part in parts)
    blocks = model // COLUMNS

    def early(phase, block):
        return jnp.where(phase == 0, block, blocks - 1)

    def late(phase, block):
        return jnp.where(phase == 0, 0, block)

    whole = [pl.BlockSpec((tokens, width), lambda p, b: (0, 0)) for width in widths]
    return pl.pallas_call(
        functools.partial(finish_kernel, widths, near, blocks),
        out_shape=jax.ShapeDtypeStruct((tokens, model), jnp.bfloat16),
        grid=(2, blocks),
        in_specs=whole
        + [
            pl.BlockSpec((COLUMNS, weight.shape[1]), lambda p, b: (early(p, b), 0)),
            pl.BlockSpec((1, COLUMNS), lambda p, b: (0, early(p, b))),
            pl.BlockSpec((near, COLUMNS), lambda p, b: (0, b)),
            pl.BlockSpec((far, COLUMNS), lambda p, b: (0, b)),
            pl.BlockSpec((tokens, COLUMNS), lambda p, b: (0, late(p, b))),
        ],
        out_specs=pl.BlockSpec((tokens, COLUMNS), lambda p, b: (0, late(p, b))),
        scratch_shapes=[
            pltpu.VMEM((blocks, tokens, COLUMNS), jnp.float32),
            pltpu.VMEM((tokens, 128), jnp.float32),
            pltpu.VMEM((tokens, 128), jnp.float32),
        ],
        compiler_params=pltpu.CompilerParams(vmem_limit_bytes=40 << 20),
        cost_estimate=pl.CostEstimate(
            flops=2 * tokens * model * weight.shape[1],
            transcendentals=0,
            bytes_accessed=2 * (model * weight.shape[1] + 4 * tokens * model),
        ),
        name="finish",
    )(*parts, weight, gain, hidden_near, hidden_far, grad_out)


def local(
    hidden, norm_gain, queries, cache, nbr_shard, nbr_slot, grad_heads, grad_out, query_weight
):
    shards = lax.axis_size("stretch")
    qwidth = queries.shape[2]
    weight_here = passed_along(query_weight[0], "section", -1)
    gain = passed_along(norm_gain, "section", -1)
    far = hidden[0, DIRECT_ROWS:]
    for _ in range(lax.axis_size("section") - 1):
        far = passed_along(far, "section", 1)
    near = passed_along(hidden[0, :DIRECT_ROWS], "section", -1)
    grads = passed_along(grad_out[0], "section", -1)

    owners = nbr_shard.reshape(-1)
    asked = owners[:, None] == jnp.arange(shards)[None, :]
    wanted = jnp.sum(jnp.where(asked, nbr_slot.reshape(-1)[:, None], 0), axis=0)
    picks = lax.all_to_all(wanted, "stretch", split_axis=0, concat_axis=0, tiled=True)
    weight_here, picks = lax.optimization_barrier((weight_here, picks))
    weight = lax.all_gather(weight_here, "stretch", axis=0, tiled=True)

    parts = []
    first_head = 0
    for heads in CHUNKS:
        first, width = first_head * HEAD_DIM, heads * HEAD_DIM
        first_head += heads
        rows = picked_rows(picks, cache[0], first, width, qwidth)
        fetched = lax.all_to_all(rows, "stretch", split_axis=0, concat_axis=0, tiled=True)
        part = query_gradient(owners, fetched, queries[0], grad_heads[0], first, heads)
        parts.append(passed_along(part, "section", -1))
    return finished(parts, weight, gain, near, far, grads)[None]


def solution(mesh):
    in_specs = (
        P("section", "stretch", None),
        P("section", None),
        P("section", "stretch", None),
        P("section", "stretch", None, None),
        P("stretch", None),
        P("stretch", None),
        P("section", "stretch", None),
        P("section", "stretch", None),
        P("section", "stretch", None),
    )
    out_specs = P("section", "stretch", None)
    return jax.shard_map(local, mesh=mesh, in_specs=in_specs, out_specs=out_specs, check_vma=False)
```

```python
import functools

import jax
import jax.numpy as jnp
from jax import lax
from jax.experimental import pallas as pl
from jax.experimental.pallas import tpu as pltpu
from jax.sharding import PartitionSpec as P

HEAD_DIM = 128
STRETCH = 64
norm_eps = 1e-05
CHUNKS = (8, 4, 4)
DIRECT_ROWS = 192
COLUMNS = 512


def passed_along(value, axis, steps):
    count = lax.axis_size(axis)
    pairs = [(source, (source + steps) % count) for source in range(count)]
    return lax.ppermute(value, axis, pairs)


def pick_kernel(key_at, value_at, width, picks, table, out, rows, arrived, left):
    groups = arrived.shape[0]
    per = rows.shape[0] // groups
    for place in range(rows.shape[0]):
        row = picks[place]
        for start, at in ((key_at, 0), (value_at, width)):
            pltpu.make_async_copy(
                table.at[row, :, pl.ds(start, width)],
                rows.at[place, :, pl.ds(at, width)],
                arrived.at[place // per],
            ).start()
    moves = []
    for group in range(groups):
        slab = pl.ds(group * per, per)
        pltpu.make_async_copy(rows.at[slab], rows.at[slab], arrived.at[group]).wait()
        moves.append(pltpu.make_async_copy(rows.at[slab], out.at[slab], left.at[group]))
        moves[-1].start()
    for move in moves:
        move.wait()


def picked_rows(picks, table, first, width, qwidth):
    places = picks.shape[0]
    span = table.shape[1]
    size = places * span * 2 * width
    groups = 4
    return pl.pallas_call(
        functools.partial(pick_kernel, first, qwidth + first, width),
        out_shape=jax.ShapeDtypeStruct((places, span, 2 * width), table.dtype),
        grid_spec=pltpu.PrefetchScalarGridSpec(
            num_scalar_prefetch=1,
            grid=(1,),
            in_specs=[pl.BlockSpec(memory_space=pl.ANY)],
            out_specs=pl.BlockSpec(memory_space=pl.ANY),
            scratch_shapes=[
                pltpu.VMEM((places, span, 2 * width), table.dtype),
                pltpu.SemaphoreType.DMA((groups,)),
                pltpu.SemaphoreType.DMA((groups,)),
            ],
        ),
        cost_estimate=pl.CostEstimate(flops=0, transcendentals=0, bytes_accessed=4 * size),
        name="pick_rows",
    )(picks, table)


def side_by_side(block, left):
    right = left + HEAD_DIM
    zeros = jnp.zeros((STRETCH, HEAD_DIM), block.dtype)
    above = jnp.concatenate([block[:, left:right], zeros], axis=1)
    below = jnp.concatenate([zeros, block[:, right : right + HEAD_DIM]], axis=1)
    return jnp.concatenate([above, below], axis=0)


def attention_kernel(heads, owners, first, second, query, grad, out):
    factor = HEAD_DIM ** (-0.5)
    width = heads * HEAD_DIM
    across = (((1,), (1,)), ((), ()))
    down = (((0,), (0,)), ((), ()))
    for left in range(0, width, 2 * HEAD_DIM):
        cols = slice(left, left + 2 * HEAD_DIM)
        vcols = slice(width + left, width + left + 2 * HEAD_DIM)
        keys = jnp.concatenate([first[0, :, cols], second[0, :, cols]], axis=0)
        values = jnp.concatenate([first[0, :, vcols], second[0, :, vcols]], axis=0)
        scores = lax.dot_general(
            keys, side_by_side(query, left), across, preferred_element_type=jnp.float32
        )
        dprob = lax.dot_general(
            values, side_by_side(grad, left), across, preferred_element_type=jnp.float32
        )
        exp_scores = jnp.exp((scores - jnp.max(scores, axis=0, keepdims=True)) * factor)
        share = 1.0 / jnp.sum(exp_scores, axis=0, keepdims=True)
        inner = jnp.sum(exp_scores * dprob, axis=0, keepdims=True) * share
        dscore = (exp_scores * (dprob - inner) * (share * factor)).astype(jnp.bfloat16)
        both = lax.dot_general(dscore, keys, down, preferred_element_type=jnp.float32)
        out[:, left : left + HEAD_DIM] = both[:STRETCH, :HEAD_DIM].astype(jnp.bfloat16)
        out[:, left + HEAD_DIM : left + 2 * HEAD_DIM] = both[STRETCH:, HEAD_DIM:].astype(
            jnp.bfloat16
        )


def query_gradient(owners, fetched, queries, grads, first, heads):
    width = heads * HEAD_DIM
    tokens = queries.shape[0]
    stretches = tokens // STRETCH
    span = fetched.shape[1]
    block = first // width
    return pl.pallas_call(
        functools.partial(attention_kernel, heads),
        out_shape=jax.ShapeDtypeStruct((tokens, width), jnp.bfloat16),
        grid_spec=pltpu.PrefetchScalarGridSpec(
            num_scalar_prefetch=1,
            grid=(stretches,),
            in_specs=[
                pl.BlockSpec((1, span, 2 * width), lambda c, own: (own[2 * c], 0, 0)),
                pl.BlockSpec((1, span, 2 * width), lambda c, own: (own[2 * c + 1], 0, 0)),
                pl.BlockSpec((STRETCH, width), lambda c, own: (c, block)),
                pl.BlockSpec((STRETCH, width), lambda c, own: (c, block)),
            ],
            out_specs=pl.BlockSpec((STRETCH, width), lambda c, own: (c, 0)),
        ),
        cost_estimate=pl.CostEstimate(
            flops=6 * tokens * STRETCH * width,
            transcendentals=tokens * STRETCH * heads,
            bytes_accessed=2 * (3 * tokens * width + 2 * stretches * span * 2 * width),
        ),
        name="query_gradient",
    )(owners, fetched, fetched, queries, grads)


def finish_kernel(widths, near, blocks, *refs):
    parts = refs[: len(widths)]
    weight, gain, hidden_near, hidden_far, grad_out, out, scaled, dots, squares = refs[len(widths) :]
    phase, block = pl.program_id(0), pl.program_id(1)
    model = blocks * COLUMNS

    @pl.when(phase == 0)
    def _():
        total = None
        start = 0
        for part, width in zip(parts, widths):
            product = lax.dot_general(
                part[...],
                weight[:, start : start + width],
                (((1,), (1,)), ((), ())),
                preferred_element_type=jnp.float32,
            )
            total = product if total is None else total + product
            start += width
        grad = total * gain[...]
        scaled[block] = grad
        for ref, rows in ((hidden_near, slice(0, near)), (hidden_far, slice(near, None))):
            values = ref[...].astype(jnp.float32)
            cross = grad[rows] * values
            square = values * values
            dot = cross[:, :128]
            norm = square[:, :128]
            for lane in range(128, COLUMNS, 128):
                dot = dot + cross[:, lane : lane + 128]
                norm = norm + square[:, lane : lane + 128]
            size = values.shape[0]
            at = pl.ds(rows.start, size)

            @pl.when(block == 0)
            def _():
                dots[at, :] = dot
                squares[at, :] = norm

            @pl.when(block > 0)
            def _():
                dots[at, :] += dot
                squares[at, :] += norm

    @pl.when((phase == 1) & (block == 0))
    def _():
        inv = lax.rsqrt(jnp.sum(squares[...], axis=-1, keepdims=True) / model + norm_eps)
        mean = inv * jnp.sum(dots[...], axis=-1, keepdims=True) / model
        squares[...] = jnp.broadcast_to(inv, squares.shape)
        dots[...] = jnp.broadcast_to(inv * inv * mean, dots.shape)

    @pl.when(phase == 1)
    def _():
        grad = scaled[block]
        for ref, rows in ((hidden_near, slice(0, near)), (hidden_far, slice(near, None))):
            size = ref.shape[0]
            at = pl.ds(rows.start, size)
            inv = squares[at, :1]
            pull = dots[at, :1]
            out[at, :] = (
                grad_out[at, :].astype(jnp.float32)
                + inv * grad[rows]
                - pull * ref[...].astype(jnp.float32)
            ).astype(out.dtype)


def finished(parts, weight, gain, hidden_near, hidden_far, grad_out):
    tokens, model = grad_out.shape
    near, far = hidden_near.shape[0], hidden_far.shape[0]
    widths = tuple(part.shape[1] for part in parts)
    blocks = model // COLUMNS

    def early(phase, block):
        return jnp.where(phase == 0, block, blocks - 1)

    def late(phase, block):
        return jnp.where(phase == 0, 0, block)

    whole = [pl.BlockSpec((tokens, width), lambda p, b: (0, 0)) for width in widths]
    return pl.pallas_call(
        functools.partial(finish_kernel, widths, near, blocks),
        out_shape=jax.ShapeDtypeStruct((tokens, model), jnp.bfloat16),
        grid=(2, blocks),
        in_specs=whole
        + [
            pl.BlockSpec((COLUMNS, weight.shape[1]), lambda p, b: (early(p, b), 0)),
            pl.BlockSpec((1, COLUMNS), lambda p, b: (0, early(p, b))),
            pl.BlockSpec((near, COLUMNS), lambda p, b: (0, b)),
            pl.BlockSpec((far, COLUMNS), lambda p, b: (0, b)),
            pl.BlockSpec((tokens, COLUMNS), lambda p, b: (0, late(p, b))),
        ],
        out_specs=pl.BlockSpec((tokens, COLUMNS), lambda p, b: (0, late(p, b))),
        scratch_shapes=[
            pltpu.VMEM((blocks, tokens, COLUMNS), jnp.float32),
            pltpu.VMEM((tokens, 128), jnp.float32),
            pltpu.VMEM((tokens, 128), jnp.float32),
        ],
        compiler_params=pltpu.CompilerParams(vmem_limit_bytes=40 << 20),
        cost_estimate=pl.CostEstimate(
            flops=2 * tokens * model * weight.shape[1],
            transcendentals=0,
            bytes_accessed=2 * (model * weight.shape[1] + 4 * tokens * model),
        ),
        name="finish",
    )(*parts, weight, gain, hidden_near, hidden_far, grad_out)


def local(
    hidden, norm_gain, queries, cache, nbr_shard, nbr_slot, grad_heads, grad_out, query_weight
):
    shards = lax.axis_size("stretch")
    qwidth = queries.shape[2]
    weight_here = passed_along(query_weight[0], "section", -1)
    gain = passed_along(norm_gain, "section", -1)
    far = hidden[0, DIRECT_ROWS:]
    for _ in range(lax.axis_size("section") - 1):
        far = passed_along(far, "section", 1)
    near = passed_along(hidden[0, :DIRECT_ROWS], "section", -1)
    grads = passed_along(grad_out[0], "section", -1)

    owners = nbr_shard.reshape(-1)
    asked = owners[:, None] == jnp.arange(shards)[None, :]
    wanted = jnp.sum(jnp.where(asked, nbr_slot.reshape(-1)[:, None], 0), axis=0)
    picks = lax.all_to_all(wanted, "stretch", split_axis=0, concat_axis=0, tiled=True)
    weight_here, picks = lax.optimization_barrier((weight_here, picks))
    weight = lax.all_gather(weight_here, "stretch", axis=0, tiled=True)

    parts = []
    first_head = 0
    for heads in CHUNKS:
        first, width = first_head * HEAD_DIM, heads * HEAD_DIM
        first_head += heads
        rows = picked_rows(picks, cache[0], first, width, qwidth)
        fetched = lax.all_to_all(rows, "stretch", split_axis=0, concat_axis=0, tiled=True)
        part = query_gradient(owners, fetched, queries[0], grad_heads[0], first, heads)
        parts.append(passed_along(part, "section", -1))
    return finished(parts, weight, gain, near, far, grads)[None]


def solution(mesh):
    in_specs = (
        P("section", "stretch", None),
        P("section", None),
        P("section", "stretch", None),
        P("section", "stretch", None, None),
        P("stretch", None),
        P("stretch", None),
        P("section", "stretch", None),
        P("section", "stretch", None),
        P("section", "stretch", None),
    )
    out_specs = P("section", "stretch", None)
    return jax.shard_map(local, mesh=mesh, in_specs=in_specs, out_specs=out_specs, check_vma=False)
```

```python
import functools

import jax
import jax.numpy as jnp
from jax import lax
from jax.experimental import pallas as pl
from jax.experimental.pallas import tpu as pltpu
from jax.sharding import PartitionSpec as P

HEAD_DIM = 128
STRETCH = 64
norm_eps = 1e-05
CHUNKS = ((0, 2), (4, 4), (8, 8), (2, 2))
HIDDEN_SPLIT = 224
GRAD_SPLIT = 368
COLUMNS = 512
VMEM = 60 << 20
SHARD = 128
STEP = 2


def passed_along(value, axis, steps):
    count = lax.axis_size(axis)
    pairs = [(source, (source + steps) % count) for source in range(count)]
    return lax.ppermute(value, axis, pairs)


def after(value, *before):
    return lax.optimization_barrier((value, *before))[0] if before else value


def pick_kernel(key_at, value_at, width, picks, table, out, rows, arrived, left):
    groups = arrived.shape[0]
    per = rows.shape[0] // groups
    for place in range(rows.shape[0]):
        row = picks[place]
        for start, at in ((key_at, 0), (value_at, width)):
            pltpu.make_async_copy(
                table.at[row, :, pl.ds(start, width)],
                rows.at[place, :, pl.ds(at, width)],
                arrived.at[place // per],
            ).start()
    moves = []
    for group in range(groups):
        slab = pl.ds(group * per, per)
        pltpu.make_async_copy(rows.at[slab], rows.at[slab], arrived.at[group]).wait()
        moves.append(pltpu.make_async_copy(rows.at[slab], out.at[slab], left.at[group]))
        moves[-1].start()
    for move in moves:
        move.wait()


def picked_rows(picks, table, first, width, qwidth):
    places = picks.shape[0]
    span = table.shape[1]
    size = places * span * 2 * width
    groups = 4
    return pl.pallas_call(
        functools.partial(pick_kernel, first, qwidth + first, width),
        out_shape=jax.ShapeDtypeStruct((places, span, 2 * width), table.dtype),
        grid_spec=pltpu.PrefetchScalarGridSpec(
            num_scalar_prefetch=1,
            grid=(1,),
            in_specs=[pl.BlockSpec(memory_space=pl.ANY)],
            out_specs=pl.BlockSpec(memory_space=pl.ANY),
            scratch_shapes=[
                pltpu.VMEM((places, span, 2 * width), table.dtype),
                pltpu.SemaphoreType.DMA((groups,)),
                pltpu.SemaphoreType.DMA((groups,)),
            ],
        ),
        compiler_params=pltpu.CompilerParams(vmem_limit_bytes=VMEM),
        cost_estimate=pl.CostEstimate(flops=0, transcendentals=0, bytes_accessed=4 * size),
        name="pick_rows",
    )(picks, table)


def side_by_side(block, left):
    right = left + HEAD_DIM
    zeros = jnp.zeros((STRETCH, HEAD_DIM), block.dtype)
    above = jnp.concatenate([block[:, left:right], zeros], axis=1)
    below = jnp.concatenate([zeros, block[:, right : right + HEAD_DIM]], axis=1)
    return jnp.concatenate([above, below], axis=0)


def attention_kernel(heads, owners, *refs):
    *rows, query, grad, out = refs
    for stretch in range(query.shape[0] // STRETCH):
        at = pl.ds(stretch * STRETCH, STRETCH)
        one_stretch(heads, *rows[2 * stretch : 2 * stretch + 2], query.at[at], grad.at[at], out.at[at])


def one_stretch(heads, first, second, query, grad, out):
    factor = HEAD_DIM ** (-0.5)
    width = heads * HEAD_DIM
    across = (((1,), (1,)), ((), ()))
    down = (((0,), (0,)), ((), ()))
    for left in range(0, width, 2 * HEAD_DIM):
        cols = slice(left, left + 2 * HEAD_DIM)
        vcols = slice(width + left, width + left + 2 * HEAD_DIM)
        keys = jnp.concatenate([first[0, :, cols], second[0, :, cols]], axis=0)
        values = jnp.concatenate([first[0, :, vcols], second[0, :, vcols]], axis=0)
        scores = lax.dot_general(
            keys, side_by_side(query, left), across, preferred_element_type=jnp.float32
        )
        dprob = lax.dot_general(
            values, side_by_side(grad, left), across, preferred_element_type=jnp.float32
        )
        exp_scores = jnp.exp((scores - jnp.max(scores, axis=0, keepdims=True)) * factor)
        share = 1.0 / jnp.sum(exp_scores, axis=0, keepdims=True)
        inner = jnp.sum(exp_scores * dprob, axis=0, keepdims=True) * share
        dscore = (exp_scores * (dprob - inner) * (share * factor)).astype(jnp.bfloat16)
        both = lax.dot_general(dscore, keys, down, preferred_element_type=jnp.float32)
        out[:, left : left + HEAD_DIM] = both[:STRETCH, :HEAD_DIM].astype(jnp.bfloat16)
        out[:, left + HEAD_DIM : left + 2 * HEAD_DIM] = both[STRETCH:, HEAD_DIM:].astype(
            jnp.bfloat16
        )


def query_gradient(owners, fetched, queries, grads, first, heads):
    width = heads * HEAD_DIM
    tokens = queries.shape[0]
    stretches = tokens // STRETCH
    span = fetched.shape[1]
    block = first // width
    rows = 2 * STEP

    def fetched_row(place):
        return pl.BlockSpec((1, span, 2 * width), lambda c, own: (own[rows * c + place], 0, 0))

    tokens_step = STEP * STRETCH
    return pl.pallas_call(
        functools.partial(attention_kernel, heads),
        out_shape=jax.ShapeDtypeStruct((tokens, width), jnp.bfloat16),
        grid_spec=pltpu.PrefetchScalarGridSpec(
            num_scalar_prefetch=1,
            grid=(stretches // STEP,),
            in_specs=[fetched_row(place) for place in range(rows)]
            + [
                pl.BlockSpec((tokens_step, width), lambda c, own: (c, block)),
                pl.BlockSpec((tokens_step, width), lambda c, own: (c, block)),
            ],
            out_specs=pl.BlockSpec((tokens_step, width), lambda c, own: (c, 0)),
        ),
        compiler_params=pltpu.CompilerParams(vmem_limit_bytes=VMEM),
        cost_estimate=pl.CostEstimate(
            flops=6 * tokens * STRETCH * width,
            transcendentals=tokens * STRETCH * heads,
            bytes_accessed=2 * (3 * tokens * width + 2 * stretches * span * 2 * width),
        ),
        name="query_gradient",
    )(owners, *([fetched] * rows), queries, grads)


def stacked(refs):
    start = 0
    for ref in refs:
        yield ref, slice(start, start + ref.shape[0])
        start += ref.shape[0]


def finish_kernel(widths, counts, blocks, core, *refs):
    refs = list(refs)
    parts, hiddens, grads = ([refs.pop(0) for _ in range(count)] for count in counts)
    own, other, gain, out, scaled, dots, squares, whole = refs
    phase, block = pl.program_id(0), pl.program_id(1)
    model = blocks * COLUMNS

    @pl.when((phase == 0) & (block == 0))
    def _():
        for part, (first, width) in zip(parts, widths):
            whole[:, first : first + width] = part[...]

    @pl.when(phase == 0)
    def _():
        totals = []
        for weight in (own, other):
            totals.append(
                lax.dot_general(
                    whole[...],
                    weight[...],
                    (((1,), (1,)), ((), ())),
                    preferred_element_type=jnp.float32,
                )
            )
        ahead = core[0] == 0
        even = jnp.where(ahead, totals[0], totals[1])
        odd = jnp.where(ahead, totals[1], totals[0])
        tiles = []
        for lane in range(0, COLUMNS // 2, SHARD):
            tiles += [even[:, lane : lane + SHARD], odd[:, lane : lane + SHARD]]
        total = jnp.concatenate(tiles, axis=1)
        grad = total * gain[...]
        scaled[block] = grad
        for ref, rows in stacked(hiddens):
            values = ref[...].astype(jnp.float32)
            cross = grad[rows] * values
            square = values * values
            dot = cross[:, :128]
            norm = square[:, :128]
            for lane in range(128, COLUMNS, 128):
                dot = dot + cross[:, lane : lane + 128]
                norm = norm + square[:, lane : lane + 128]
            at = rows

            @pl.when(block == 0)
            def _():
                dots[at, :] = dot
                squares[at, :] = norm

            @pl.when(block > 0)
            def _():
                dots[at, :] += dot
                squares[at, :] += norm

    @pl.when((phase == 1) & (block == 0))
    def _():
        inv = lax.rsqrt(jnp.sum(squares[...], axis=-1, keepdims=True) / model + norm_eps)
        mean = inv * jnp.sum(dots[...], axis=-1, keepdims=True) / model
        squares[...] = jnp.broadcast_to(inv, squares.shape)
        dots[...] = jnp.broadcast_to(inv * inv * mean, dots.shape)

    @pl.when(phase == 1)
    def _():
        grad = scaled.at[block]
        across = COLUMNS // 128
        for values, rows in stacked(hiddens):
            for added, others in stacked(grads):
                start, stop = max(rows.start, others.start), min(rows.stop, others.stop)
                if start < stop:
                    at = slice(start, stop)
                    held = values[start - rows.start : stop - rows.start]
                    sent = added[start - others.start : stop - others.start]
                    inv = jnp.concatenate([squares[at, :]] * across, axis=1)
                    pull = jnp.concatenate([dots[at, :]] * across, axis=1)
                    out[at, :] = (
                        sent.astype(jnp.float32)
                        + inv * grad[at]
                        - pull * held.astype(jnp.float32)
                    ).astype(out.dtype)


def finished(parts, hiddens, grads, own, other, core, gain):
    tokens = sum(piece.shape[0] for piece in grads)
    model = gain.shape[1]
    widths = tuple((first * HEAD_DIM, heads * HEAD_DIM) for first, heads in CHUNKS)
    blocks = model // COLUMNS
    qwidth = own.shape[1]

    def early(phase, block):
        return jnp.where(phase == 0, block, blocks - 1)

    def late(phase, block):
        return jnp.where(phase == 0, 0, block)

    whole = [pl.BlockSpec((tokens, width), lambda p, b, c: (0, 0)) for _, width in widths]
    return pl.pallas_call(
        functools.partial(finish_kernel, widths, tuple(map(len, (parts, hiddens, grads))), blocks),
        out_shape=jax.ShapeDtypeStruct((tokens, model), jnp.bfloat16),
        grid_spec=pltpu.PrefetchScalarGridSpec(
            num_scalar_prefetch=1,
            grid=(2, blocks),
            in_specs=whole
            + [pl.BlockSpec((piece.shape[0], COLUMNS), lambda p, b, c: (0, b)) for piece in hiddens]
            + [
                pl.BlockSpec((piece.shape[0], COLUMNS), lambda p, b, c: (0, late(p, b)))
                for piece in grads
            ]
            + [pl.BlockSpec((COLUMNS // 2, qwidth), lambda p, b, c: (early(p, b), 0))] * 2
            + [pl.BlockSpec((1, COLUMNS), lambda p, b, c: (0, early(p, b)))],
            out_specs=pl.BlockSpec((tokens, COLUMNS), lambda p, b, c: (0, late(p, b))),
            scratch_shapes=[
                pltpu.VMEM((blocks, tokens, COLUMNS), jnp.float32),
                pltpu.VMEM((tokens, 128), jnp.float32),
                pltpu.VMEM((tokens, 128), jnp.float32),
                pltpu.VMEM((tokens, qwidth), jnp.bfloat16),
            ],
        ),
        compiler_params=pltpu.CompilerParams(vmem_limit_bytes=VMEM),
        cost_estimate=pl.CostEstimate(
            flops=2 * tokens * model * qwidth,
            transcendentals=0,
            bytes_accessed=2 * (model * qwidth + 4 * tokens * model),
        ),
        name="finish",
    )(core, *parts, *hiddens, *grads, own, other, gain)


def local(
    hidden, norm_gain, queries, cache, nbr_shard, nbr_slot, grad_heads, grad_out, query_weight
):
    shards = lax.axis_size("stretch")
    qwidth = queries.shape[2]
    together = lax.optimization_barrier

    def back(value):
        return passed_along(value, "section", -1)

    def ahead(value):
        return passed_along(value, "section", 1)

    def picked(chunk, picks):
        first_head, heads = CHUNKS[chunk]
        return picked_rows(picks, cache[0], first_head * HEAD_DIM, heads * HEAD_DIM, qwidth)

    def exchanged(rows):
        return lax.all_to_all(rows, "stretch", split_axis=0, concat_axis=0, tiled=True)

    def gradient(chunk, fetched):
        first_head, heads = CHUNKS[chunk]
        return query_gradient(
            owners, fetched, queries[0], grad_heads[0], first_head * HEAD_DIM, heads
        )

    here = hidden[0], grad_out[0]
    near = HIDDEN_SPLIT
    owners = nbr_shard.reshape(-1)
    asked = owners[:, None] == jnp.arange(shards)[None, :]
    wanted = jnp.sum(jnp.where(asked, nbr_slot.reshape(-1)[:, None], 0), axis=0)
    core = lax.rem(lax.axis_index("stretch"), 2).reshape(1)

    gain, weight_here = back(norm_gain), back(query_weight[0])
    hidden_near, far = back(here[0][:near]), ahead(here[0][near:])
    grads_soon = back(here[1][:GRAD_SPLIT])
    weight_here, wanted = together((weight_here, wanted))
    kinds = [list(range(kind, shards, 2)) for kind in range(2)]
    own = lax.all_gather(weight_here, "stretch", axis=0, tiled=True, axis_index_groups=kinds)
    picks = lax.all_to_all(wanted, "stretch", split_axis=0, concat_axis=0, tiled=True)
    picks, core = together((picks, core))
    rows = picked(0, picks)
    fetched = exchanged(rows)
    rows = picked(1, after(picks, rows))

    hidden_near, far, rows, picks, fetched = together((hidden_near, far, rows, picks, fetched))
    far = ahead(far)
    local0 = gradient(0, fetched)
    fetched = exchanged(rows)
    rows = picked(2, picks)

    here, gain, grads_soon, far, rows, picks, fetched, local0 = together(
        (here, gain, grads_soon, far, rows, picks, fetched, local0)
    )
    far, grads, part0 = ahead(far), back(here[1][GRAD_SPLIT:]), back(local0)
    local1 = gradient(1, fetched)
    fetched = exchanged(rows)
    rows = picked(3, picks)
    part1 = back(local1)

    rows, fetched, own, grads, far, part0, part1 = together(
        (rows, fetched, own, grads, far, part0, part1)
    )
    local2 = gradient(2, fetched)
    fetched = exchanged(rows)
    part2 = back(local2)
    other = lax.ppermute(own, "stretch", [(place, place ^ 1) for place in range(shards)])

    local2, fetched = together((local2, fetched))
    part3 = back(gradient(3, fetched))
    return finished(
        (part0, part1, part2, part3),
        (hidden_near, far),
        (grads_soon, grads),
        own,
        other,
        core,
        gain,
    )[None]


def solution(mesh):
    in_specs = (
        P("section", "stretch", None),
        P("section", None),
        P("section", "stretch", None),
        P("section", "stretch", None, None),
        P("stretch", None),
        P("stretch", None),
        P("section", "stretch", None),
        P("section", "stretch", None),
        P("section", "stretch", None),
    )
    out_specs = P("section", "stretch", None)
    return jax.shard_map(local, mesh=mesh, in_specs=in_specs, out_specs=out_specs, check_vma=False)
```

```python
import functools

import jax
import jax.numpy as jnp
from jax import lax
from jax.experimental import pallas as pl
from jax.experimental.pallas import tpu as pltpu
from jax.sharding import PartitionSpec as P

HEAD_DIM = 128
STRETCH = 64
norm_eps = 1e-05
CHUNKS = ((0, 2), (4, 4), (8, 8), (2, 2))
HIDDEN_SPLIT = 224
GRAD_SPLIT = 368
PARTS = ((0, 2), (4, 4), (8, 4), (12, 4), (2, 2))
COLUMNS = 1024
VMEM = 60 << 20
SHARD = 128
STEP = 2


def passed_along(value, axis, steps):
    count = lax.axis_size(axis)
    pairs = [(source, (source + steps) % count) for source in range(count)]
    return lax.ppermute(value, axis, pairs)


def after(value, *before):
    return lax.optimization_barrier((value, *before))[0] if before else value


def pick_kernel(key_at, value_at, width, picks, table, out, rows, arrived, left):
    groups = arrived.shape[0]
    per = rows.shape[0] // groups
    for place in range(rows.shape[0]):
        row = picks[place]
        for start, at in ((key_at, 0), (value_at, width)):
            pltpu.make_async_copy(
                table.at[row, :, pl.ds(start, width)],
                rows.at[place, :, pl.ds(at, width)],
                arrived.at[place // per],
            ).start()
    moves = []
    for group in range(groups):
        slab = pl.ds(group * per, per)
        pltpu.make_async_copy(rows.at[slab], rows.at[slab], arrived.at[group]).wait()
        moves.append(pltpu.make_async_copy(rows.at[slab], out.at[slab], left.at[group]))
        moves[-1].start()
    for move in moves:
        move.wait()


def picked_rows(picks, table, first, width, qwidth):
    places = picks.shape[0]
    span = table.shape[1]
    size = places * span * 2 * width
    groups = 4
    return pl.pallas_call(
        functools.partial(pick_kernel, first, qwidth + first, width),
        out_shape=jax.ShapeDtypeStruct((places, span, 2 * width), table.dtype),
        grid_spec=pltpu.PrefetchScalarGridSpec(
            num_scalar_prefetch=1,
            grid=(1,),
            in_specs=[pl.BlockSpec(memory_space=pl.ANY)],
            out_specs=pl.BlockSpec(memory_space=pl.ANY),
            scratch_shapes=[
                pltpu.VMEM((places, span, 2 * width), table.dtype),
                pltpu.SemaphoreType.DMA((groups,)),
                pltpu.SemaphoreType.DMA((groups,)),
            ],
        ),
        compiler_params=pltpu.CompilerParams(vmem_limit_bytes=VMEM),
        cost_estimate=pl.CostEstimate(flops=0, transcendentals=0, bytes_accessed=4 * size),
        name="pick_rows",
    )(picks, table)


def side_by_side(block, left):
    right = left + HEAD_DIM
    zeros = jnp.zeros((STRETCH, HEAD_DIM), block.dtype)
    above = jnp.concatenate([block[:, left:right], zeros], axis=1)
    below = jnp.concatenate([zeros, block[:, right : right + HEAD_DIM]], axis=1)
    return jnp.concatenate([above, below], axis=0)


def attention_kernel(heads, owners, *refs):
    *rows, query, grad, out = refs
    for stretch in range(query.shape[0] // STRETCH):
        at = pl.ds(stretch * STRETCH, STRETCH)
        one_stretch(heads, *rows[4 * stretch : 4 * stretch + 4], query.at[at], grad.at[at], out.at[at])


def one_stretch(heads, first_keys, first_values, second_keys, second_values, query, grad, out):
    factor = HEAD_DIM ** (-0.5)
    width = heads * HEAD_DIM
    across = (((1,), (1,)), ((), ()))
    down = (((0,), (0,)), ((), ()))
    for left in range(0, width, 2 * HEAD_DIM):
        cols = slice(left, left + 2 * HEAD_DIM)
        keys = jnp.concatenate([first_keys[0, :, cols], second_keys[0, :, cols]], axis=0)
        values = jnp.concatenate([first_values[0, :, cols], second_values[0, :, cols]], axis=0)
        scores = lax.dot_general(
            keys, side_by_side(query, left), across, preferred_element_type=jnp.float32
        )
        dprob = lax.dot_general(
            values, side_by_side(grad, left), across, preferred_element_type=jnp.float32
        )
        exp_scores = jnp.exp((scores - jnp.max(scores, axis=0, keepdims=True)) * factor)
        share = 1.0 / jnp.sum(exp_scores, axis=0, keepdims=True)
        inner = jnp.sum(exp_scores * dprob, axis=0, keepdims=True) * share
        dscore = (exp_scores * (dprob - inner) * (share * factor)).astype(jnp.bfloat16)
        both = lax.dot_general(dscore, keys, down, preferred_element_type=jnp.float32)
        out[:, left : left + HEAD_DIM] = both[:STRETCH, :HEAD_DIM].astype(jnp.bfloat16)
        out[:, left + HEAD_DIM : left + 2 * HEAD_DIM] = both[STRETCH:, HEAD_DIM:].astype(
            jnp.bfloat16
        )


def query_gradient(owners, fetched, queries, grads, first, heads, skipped=0):
    width = heads * HEAD_DIM
    tokens = queries.shape[0]
    stretches = tokens // STRETCH
    span = fetched.shape[1]
    block = first // width
    rows = 2 * STEP

    within = fetched.shape[2] // (2 * width)

    def fetched_row(place, kind):
        return pl.BlockSpec(
            (1, span, width),
            lambda c, own: (own[rows * c + place], 0, kind * within + skipped // width),
        )

    tokens_step = STEP * STRETCH
    return pl.pallas_call(
        functools.partial(attention_kernel, heads),
        out_shape=jax.ShapeDtypeStruct((tokens, width), jnp.bfloat16),
        grid_spec=pltpu.PrefetchScalarGridSpec(
            num_scalar_prefetch=1,
            grid=(stretches // STEP,),
            in_specs=[fetched_row(place, kind) for place in range(rows) for kind in range(2)]
            + [
                pl.BlockSpec((tokens_step, width), lambda c, own: (c, block)),
                pl.BlockSpec((tokens_step, width), lambda c, own: (c, block)),
            ],
            out_specs=pl.BlockSpec((tokens_step, width), lambda c, own: (c, 0)),
        ),
        compiler_params=pltpu.CompilerParams(vmem_limit_bytes=VMEM),
        cost_estimate=pl.CostEstimate(
            flops=6 * tokens * STRETCH * width,
            transcendentals=tokens * STRETCH * heads,
            bytes_accessed=2 * (3 * tokens * width + 2 * stretches * span * 2 * width),
        ),
        name="query_gradient",
    )(owners, *([fetched] * (2 * rows)), queries, grads)


def stacked(refs):
    start = 0
    for ref in refs:
        yield ref, slice(start, start + ref.shape[0])
        start += ref.shape[0]


def finish_kernel(widths, counts, blocks, core, *refs):
    refs = list(refs)
    parts, hiddens, grads = ([refs.pop(0) for _ in range(count)] for count in counts)
    own, other, gain, out, scaled, dots, squares, whole = refs
    phase, block = pl.program_id(0), pl.program_id(1)
    model = blocks * COLUMNS

    @pl.when((phase == 0) & (block == 0))
    def _():
        for part, (first, width) in zip(parts, widths):
            whole[:, first : first + width] = part[...]

    @pl.when(phase == 0)
    def _():
        totals = []
        for weight in (own, other):
            totals.append(
                lax.dot_general(
                    whole[...],
                    weight[...],
                    (((1,), (1,)), ((), ())),
                    preferred_element_type=jnp.float32,
                )
            )
        ahead = core[0] == 0
        even = jnp.where(ahead, totals[0], totals[1])
        odd = jnp.where(ahead, totals[1], totals[0])
        tiles = []
        for lane in range(0, COLUMNS // 2, SHARD):
            tiles += [even[:, lane : lane + SHARD], odd[:, lane : lane + SHARD]]
        total = jnp.concatenate(tiles, axis=1)
        grad = total * gain[...]
        scaled[block] = grad
        for ref, rows in stacked(hiddens):
            values = ref[...].astype(jnp.float32)
            cross = grad[rows] * values
            square = values * values
            dot = cross[:, :128]
            norm = square[:, :128]
            for lane in range(128, COLUMNS, 128):
                dot = dot + cross[:, lane : lane + 128]
                norm = norm + square[:, lane : lane + 128]
            at = rows

            @pl.when(block == 0)
            def _():
                dots[at, :] = dot
                squares[at, :] = norm

            @pl.when(block > 0)
            def _():
                dots[at, :] += dot
                squares[at, :] += norm

    @pl.when((phase == 1) & (block == 0))
    def _():
        inv = lax.rsqrt(jnp.sum(squares[...], axis=-1, keepdims=True) / model + norm_eps)
        mean = inv * jnp.sum(dots[...], axis=-1, keepdims=True) / model
        squares[...] = jnp.broadcast_to(inv, squares.shape)
        dots[...] = jnp.broadcast_to(inv * inv * mean, dots.shape)

    @pl.when(phase == 1)
    def _():
        grad = scaled.at[block]
        across = COLUMNS // 128
        for values, rows in stacked(hiddens):
            for added, others in stacked(grads):
                start, stop = max(rows.start, others.start), min(rows.stop, others.stop)
                if start < stop:
                    at = slice(start, stop)
                    held = values[start - rows.start : stop - rows.start]
                    sent = added[start - others.start : stop - others.start]
                    inv = jnp.concatenate([squares[at, :]] * across, axis=1)
                    pull = jnp.concatenate([dots[at, :]] * across, axis=1)
                    out[at, :] = (
                        sent.astype(jnp.float32)
                        + inv * grad[at]
                        - pull * held.astype(jnp.float32)
                    ).astype(out.dtype)


def finished(parts, hiddens, grads, own, other, core, gain):
    tokens = sum(piece.shape[0] for piece in grads)
    model = gain.shape[1]
    widths = tuple((first * HEAD_DIM, heads * HEAD_DIM) for first, heads in PARTS)
    blocks = model // COLUMNS
    qwidth = own.shape[1]

    def early(phase, block):
        return jnp.where(phase == 0, block, blocks - 1)

    def late(phase, block):
        return jnp.where(phase == 0, 0, block)

    whole = [pl.BlockSpec((tokens, width), lambda p, b, c: (0, 0)) for _, width in widths]
    return pl.pallas_call(
        functools.partial(finish_kernel, widths, tuple(map(len, (parts, hiddens, grads))), blocks),
        out_shape=jax.ShapeDtypeStruct((tokens, model), jnp.bfloat16),
        grid_spec=pltpu.PrefetchScalarGridSpec(
            num_scalar_prefetch=1,
            grid=(2, blocks),
            in_specs=whole
            + [pl.BlockSpec((piece.shape[0], COLUMNS), lambda p, b, c: (0, b)) for piece in hiddens]
            + [
                pl.BlockSpec((piece.shape[0], COLUMNS), lambda p, b, c: (0, late(p, b)))
                for piece in grads
            ]
            + [pl.BlockSpec((COLUMNS // 2, qwidth), lambda p, b, c: (early(p, b), 0))] * 2
            + [pl.BlockSpec((1, COLUMNS), lambda p, b, c: (0, early(p, b)))],
            out_specs=pl.BlockSpec((tokens, COLUMNS), lambda p, b, c: (0, late(p, b))),
            scratch_shapes=[
                pltpu.VMEM((blocks, tokens, COLUMNS), jnp.float32),
                pltpu.VMEM((tokens, 128), jnp.float32),
                pltpu.VMEM((tokens, 128), jnp.float32),
                pltpu.VMEM((tokens, qwidth), jnp.bfloat16),
            ],
        ),
        compiler_params=pltpu.CompilerParams(vmem_limit_bytes=VMEM),
        cost_estimate=pl.CostEstimate(
            flops=2 * tokens * model * qwidth,
            transcendentals=0,
            bytes_accessed=2 * (model * qwidth + 4 * tokens * model),
        ),
        name="finish",
    )(core, *parts, *hiddens, *grads, own, other, gain)


def local(
    hidden, norm_gain, queries, cache, nbr_shard, nbr_slot, grad_heads, grad_out, query_weight
):
    shards = lax.axis_size("stretch")
    qwidth = queries.shape[2]
    together = lax.optimization_barrier

    def back(value):
        return passed_along(value, "section", -1)

    def ahead(value):
        return passed_along(value, "section", 1)

    def picked(chunk, picks):
        first_head, heads = CHUNKS[chunk]
        return picked_rows(picks, cache[0], first_head * HEAD_DIM, heads * HEAD_DIM, qwidth)

    def exchanged(rows):
        return lax.all_to_all(rows, "stretch", split_axis=0, concat_axis=0, tiled=True)

    def gradient(chunk, fetched):
        first_head, heads = CHUNKS[chunk]
        return query_gradient(
            owners, fetched, queries[0], grad_heads[0], first_head * HEAD_DIM, heads
        )

    here = hidden[0], grad_out[0]
    near = HIDDEN_SPLIT
    owners = nbr_shard.reshape(-1)
    asked = owners[:, None] == jnp.arange(shards)[None, :]
    wanted = jnp.sum(jnp.where(asked, nbr_slot.reshape(-1)[:, None], 0), axis=0)
    core = lax.rem(lax.axis_index("stretch"), 2).reshape(1)

    gain, weight_here = back(norm_gain), back(query_weight[0])
    hidden_near, far = back(here[0][:near]), ahead(here[0][near:])
    grads_soon = back(here[1][:GRAD_SPLIT])
    weight_here, wanted = together((weight_here, wanted))
    kinds = [list(range(kind, shards, 2)) for kind in range(2)]
    own = lax.all_gather(weight_here, "stretch", axis=0, tiled=True, axis_index_groups=kinds)
    picks = lax.all_to_all(wanted, "stretch", split_axis=0, concat_axis=0, tiled=True)
    picks, core = together((picks, core))
    rows = picked(0, picks)
    fetched = exchanged(rows)
    rows = picked(1, after(picks, rows))

    hidden_near, far, rows, picks, fetched = together((hidden_near, far, rows, picks, fetched))
    far = ahead(far)
    local0 = gradient(0, fetched)
    fetched = exchanged(rows)
    rows = picked(2, picks)

    here, gain, grads_soon, far, rows, picks, fetched, local0 = together(
        (here, gain, grads_soon, far, rows, picks, fetched, local0)
    )
    far, grads, part0 = ahead(far), back(here[1][GRAD_SPLIT:]), back(local0)
    local1 = gradient(1, fetched)
    fetched = exchanged(rows)
    rows = picked(3, picks)
    part1 = back(local1)

    rows, fetched, own, grads, far, part0, part1 = together(
        (rows, fetched, own, grads, far, part0, part1)
    )
    held = fetched
    local2 = query_gradient(owners, held, queries[0], grad_heads[0], 8 * HEAD_DIM, 4)
    fetched = exchanged(rows)
    part2 = back(local2)
    local3 = query_gradient(
        owners, after(held, local2), queries[0], grad_heads[0], 12 * HEAD_DIM, 4, 4 * HEAD_DIM
    )
    part3 = back(local3)
    other = lax.ppermute(own, "stretch", [(place, place ^ 1) for place in range(shards)])

    local3, part2, fetched = together((local3, part2, fetched))
    part4 = back(gradient(3, fetched))
    return finished(
        (part0, part1, part2, part3, part4),
        (hidden_near, far),
        (grads_soon, grads),
        own,
        other,
        core,
        gain,
    )[None]


def solution(mesh):
    in_specs = (
        P("section", "stretch", None),
        P("section", None),
        P("section", "stretch", None),
        P("section", "stretch", None, None),
        P("stretch", None),
        P("stretch", None),
        P("section", "stretch", None),
        P("section", "stretch", None),
        P("section", "stretch", None),
    )
    out_specs = P("section", "stretch", None)
    return jax.shard_map(local, mesh=mesh, in_specs=in_specs, out_specs=out_specs, check_vma=False)
```

```python
import functools

import jax
import jax.numpy as jnp
from jax import lax
from jax.experimental import pallas as pl
from jax.experimental.pallas import tpu as pltpu
from jax.sharding import PartitionSpec as P

HEAD_DIM = 128
STRETCH = 64
norm_eps = 1e-05
CHUNKS = ((0, 2), (4, 4), (8, 8), (2, 2))
HIDDEN_SPLIT = 240
GRAD_SPLIT = 352
PARTS = ((0, 2), (4, 4), (8, 4), (12, 4), (2, 2))
COLUMNS = 1024
VMEM = 60 << 20
SHARD = 128
STEP = 2


def passed_along(value, axis, steps):
    count = lax.axis_size(axis)
    pairs = [(source, (source + steps) % count) for source in range(count)]
    return lax.ppermute(value, axis, pairs)


def after(value, *before):
    return lax.optimization_barrier((value, *before))[0] if before else value


def pick_kernel(key_at, value_at, width, picks, table, out, rows, arrived, left):
    groups = arrived.shape[0]
    per = rows.shape[0] // groups
    for place in range(rows.shape[0]):
        row = picks[place]
        for start, at in ((key_at, 0), (value_at, width)):
            pltpu.make_async_copy(
                table.at[row, :, pl.ds(start, width)],
                rows.at[place, :, pl.ds(at, width)],
                arrived.at[place // per],
            ).start()
    moves = []
    for group in range(groups):
        slab = pl.ds(group * per, per)
        pltpu.make_async_copy(rows.at[slab], rows.at[slab], arrived.at[group]).wait()
        moves.append(pltpu.make_async_copy(rows.at[slab], out.at[slab], left.at[group]))
        moves[-1].start()
    for move in moves:
        move.wait()


def picked_rows(picks, table, first, width, qwidth):
    places = picks.shape[0]
    span = table.shape[1]
    size = places * span * 2 * width
    groups = 4
    return pl.pallas_call(
        functools.partial(pick_kernel, first, qwidth + first, width),
        out_shape=jax.ShapeDtypeStruct((places, span, 2 * width), table.dtype),
        grid_spec=pltpu.PrefetchScalarGridSpec(
            num_scalar_prefetch=1,
            grid=(1,),
            in_specs=[pl.BlockSpec(memory_space=pl.ANY)],
            out_specs=pl.BlockSpec(memory_space=pl.ANY),
            scratch_shapes=[
                pltpu.VMEM((places, span, 2 * width), table.dtype),
                pltpu.SemaphoreType.DMA((groups,)),
                pltpu.SemaphoreType.DMA((groups,)),
            ],
        ),
        compiler_params=pltpu.CompilerParams(vmem_limit_bytes=VMEM),
        cost_estimate=pl.CostEstimate(flops=0, transcendentals=0, bytes_accessed=4 * size),
        name="pick_rows",
    )(picks, table)


def side_by_side(block, left):
    right = left + HEAD_DIM
    zeros = jnp.zeros((STRETCH, HEAD_DIM), block.dtype)
    above = jnp.concatenate([block[:, left:right], zeros], axis=1)
    below = jnp.concatenate([zeros, block[:, right : right + HEAD_DIM]], axis=1)
    return jnp.concatenate([above, below], axis=0)


def attention_kernel(heads, owners, *refs):
    *rows, query, grad, out = refs
    for stretch in range(query.shape[0] // STRETCH):
        at = pl.ds(stretch * STRETCH, STRETCH)
        one_stretch(heads, *rows[4 * stretch : 4 * stretch + 4], query.at[at], grad.at[at], out.at[at])


def one_stretch(heads, first_keys, first_values, second_keys, second_values, query, grad, out):
    factor = HEAD_DIM ** (-0.5)
    width = heads * HEAD_DIM
    across = (((1,), (1,)), ((), ()))
    down = (((0,), (0,)), ((), ()))
    for left in range(0, width, 2 * HEAD_DIM):
        cols = slice(left, left + 2 * HEAD_DIM)
        keys = jnp.concatenate([first_keys[0, :, cols], second_keys[0, :, cols]], axis=0)
        values = jnp.concatenate([first_values[0, :, cols], second_values[0, :, cols]], axis=0)
        scores = lax.dot_general(
            keys, side_by_side(query, left), across, preferred_element_type=jnp.float32
        )
        dprob = lax.dot_general(
            values, side_by_side(grad, left), across, preferred_element_type=jnp.float32
        )
        exp_scores = jnp.exp((scores - jnp.max(scores, axis=0, keepdims=True)) * factor)
        share = 1.0 / jnp.sum(exp_scores, axis=0, keepdims=True)
        inner = jnp.sum(exp_scores * dprob, axis=0, keepdims=True) * share
        dscore = (exp_scores * (dprob - inner) * (share * factor)).astype(jnp.bfloat16)
        both = lax.dot_general(dscore, keys, down, preferred_element_type=jnp.float32)
        out[:, left : left + HEAD_DIM] = both[:STRETCH, :HEAD_DIM].astype(jnp.bfloat16)
        out[:, left + HEAD_DIM : left + 2 * HEAD_DIM] = both[STRETCH:, HEAD_DIM:].astype(
            jnp.bfloat16
        )


def query_gradient(owners, fetched, queries, grads, first, heads, skipped=0):
    width = heads * HEAD_DIM
    tokens = queries.shape[0]
    stretches = tokens // STRETCH
    span = fetched.shape[1]
    block = first // width
    rows = 2 * STEP

    within = fetched.shape[2] // (2 * width)

    def fetched_row(place, kind):
        return pl.BlockSpec(
            (1, span, width),
            lambda c, own: (own[rows * c + place], 0, kind * within + skipped // width),
        )

    tokens_step = STEP * STRETCH
    return pl.pallas_call(
        functools.partial(attention_kernel, heads),
        out_shape=jax.ShapeDtypeStruct((tokens, width), jnp.bfloat16),
        grid_spec=pltpu.PrefetchScalarGridSpec(
            num_scalar_prefetch=1,
            grid=(stretches // STEP,),
            in_specs=[fetched_row(place, kind) for place in range(rows) for kind in range(2)]
            + [
                pl.BlockSpec((tokens_step, width), lambda c, own: (c, block)),
                pl.BlockSpec((tokens_step, width), lambda c, own: (c, block)),
            ],
            out_specs=pl.BlockSpec((tokens_step, width), lambda c, own: (c, 0)),
        ),
        compiler_params=pltpu.CompilerParams(vmem_limit_bytes=VMEM),
        cost_estimate=pl.CostEstimate(
            flops=6 * tokens * STRETCH * width,
            transcendentals=tokens * STRETCH * heads,
            bytes_accessed=2 * (3 * tokens * width + 2 * stretches * span * 2 * width),
        ),
        name="query_gradient",
    )(owners, *([fetched] * (2 * rows)), queries, grads)


def stacked(refs):
    start = 0
    for ref in refs:
        yield ref, slice(start, start + ref.shape[0])
        start += ref.shape[0]


def finish_kernel(widths, counts, blocks, core, *refs):
    refs = list(refs)
    parts, hiddens, grads = ([refs.pop(0) for _ in range(count)] for count in counts)
    own, other, gain, out, scaled, dots, squares, whole = refs
    phase, block = pl.program_id(0), pl.program_id(1)
    model = blocks * COLUMNS

    @pl.when((phase == 0) & (block == 0))
    def _():
        for part, (first, width) in zip(parts, widths):
            whole[:, first : first + width] = part[...]

    @pl.when(phase == 0)
    def _():
        totals = []
        for weight in (own, other):
            totals.append(
                lax.dot_general(
                    whole[...],
                    weight[...],
                    (((1,), (1,)), ((), ())),
                    preferred_element_type=jnp.float32,
                )
            )
        ahead = core[0] == 0
        even = jnp.where(ahead, totals[0], totals[1])
        odd = jnp.where(ahead, totals[1], totals[0])
        tiles = []
        for lane in range(0, COLUMNS // 2, SHARD):
            tiles += [even[:, lane : lane + SHARD], odd[:, lane : lane + SHARD]]
        total = jnp.concatenate(tiles, axis=1)
        grad = total * gain[...]
        scaled[block] = grad
        for ref, rows in stacked(hiddens):
            values = ref[...].astype(jnp.float32)
            cross = grad[rows] * values
            square = values * values
            dot = cross[:, :128]
            norm = square[:, :128]
            for lane in range(128, COLUMNS, 128):
                dot = dot + cross[:, lane : lane + 128]
                norm = norm + square[:, lane : lane + 128]
            at = rows

            @pl.when(block == 0)
            def _():
                dots[at, :] = dot
                squares[at, :] = norm

            @pl.when(block > 0)
            def _():
                dots[at, :] += dot
                squares[at, :] += norm

    @pl.when((phase == 1) & (block == 0))
    def _():
        inv = lax.rsqrt(jnp.sum(squares[...], axis=-1, keepdims=True) / model + norm_eps)
        mean = inv * jnp.sum(dots[...], axis=-1, keepdims=True) / model
        squares[...] = jnp.broadcast_to(inv, squares.shape)
        dots[...] = jnp.broadcast_to(inv * inv * mean, dots.shape)

    @pl.when(phase == 1)
    def _():
        grad = scaled.at[block]
        across = COLUMNS // 128
        for values, rows in stacked(hiddens):
            for added, others in stacked(grads):
                start, stop = max(rows.start, others.start), min(rows.stop, others.stop)
                if start < stop:
                    at = slice(start, stop)
                    held = values[start - rows.start : stop - rows.start]
                    sent = added[start - others.start : stop - others.start]
                    inv = jnp.concatenate([squares[at, :]] * across, axis=1)
                    pull = jnp.concatenate([dots[at, :]] * across, axis=1)
                    out[at, :] = (
                        sent.astype(jnp.float32)
                        + inv * grad[at]
                        - pull * held.astype(jnp.float32)
                    ).astype(out.dtype)


def finished(parts, hiddens, grads, own, other, core, gain):
    tokens = sum(piece.shape[0] for piece in grads)
    model = gain.shape[1]
    widths = tuple((first * HEAD_DIM, heads * HEAD_DIM) for first, heads in PARTS)
    blocks = model // COLUMNS
    qwidth = own.shape[1]

    def early(phase, block):
        return jnp.where(phase == 0, block, blocks - 1)

    def late(phase, block):
        return jnp.where(phase == 0, 0, block)

    whole = [pl.BlockSpec((tokens, width), lambda p, b, c: (0, 0)) for _, width in widths]
    return pl.pallas_call(
        functools.partial(finish_kernel, widths, tuple(map(len, (parts, hiddens, grads))), blocks),
        out_shape=jax.ShapeDtypeStruct((tokens, model), jnp.bfloat16),
        grid_spec=pltpu.PrefetchScalarGridSpec(
            num_scalar_prefetch=1,
            grid=(2, blocks),
            in_specs=whole
            + [pl.BlockSpec((piece.shape[0], COLUMNS), lambda p, b, c: (0, b)) for piece in hiddens]
            + [
                pl.BlockSpec((piece.shape[0], COLUMNS), lambda p, b, c: (0, late(p, b)))
                for piece in grads
            ]
            + [pl.BlockSpec((COLUMNS // 2, qwidth), lambda p, b, c: (early(p, b), 0))] * 2
            + [pl.BlockSpec((1, COLUMNS), lambda p, b, c: (0, early(p, b)))],
            out_specs=pl.BlockSpec((tokens, COLUMNS), lambda p, b, c: (0, late(p, b))),
            scratch_shapes=[
                pltpu.VMEM((blocks, tokens, COLUMNS), jnp.float32),
                pltpu.VMEM((tokens, 128), jnp.float32),
                pltpu.VMEM((tokens, 128), jnp.float32),
                pltpu.VMEM((tokens, qwidth), jnp.bfloat16),
            ],
        ),
        compiler_params=pltpu.CompilerParams(vmem_limit_bytes=VMEM),
        cost_estimate=pl.CostEstimate(
            flops=2 * tokens * model * qwidth,
            transcendentals=0,
            bytes_accessed=2 * (model * qwidth + 4 * tokens * model),
        ),
        name="finish",
    )(core, *parts, *hiddens, *grads, own, other, gain)


def local(
    hidden, norm_gain, queries, cache, nbr_shard, nbr_slot, grad_heads, grad_out, query_weight
):
    shards = lax.axis_size("stretch")
    qwidth = queries.shape[2]
    together = lax.optimization_barrier

    def back(value):
        return passed_along(value, "section", -1)

    def ahead(value):
        return passed_along(value, "section", 1)

    def picked(chunk, picks):
        first_head, heads = CHUNKS[chunk]
        return picked_rows(picks, cache[0], first_head * HEAD_DIM, heads * HEAD_DIM, qwidth)

    def exchanged(rows):
        return lax.all_to_all(rows, "stretch", split_axis=0, concat_axis=0, tiled=True)

    def gradient(chunk, fetched):
        first_head, heads = CHUNKS[chunk]
        return query_gradient(
            owners, fetched, queries[0], grad_heads[0], first_head * HEAD_DIM, heads
        )

    here = hidden[0], grad_out[0]
    near = HIDDEN_SPLIT
    owners = nbr_shard.reshape(-1)
    asked = owners[:, None] == jnp.arange(shards)[None, :]
    wanted = jnp.sum(jnp.where(asked, nbr_slot.reshape(-1)[:, None], 0), axis=0)
    core = lax.rem(lax.axis_index("stretch"), 2).reshape(1)

    gain, weight_here = back(norm_gain), back(query_weight[0])
    hidden_near, far = back(here[0][:near]), ahead(here[0][near:])
    grads_soon = back(here[1][:GRAD_SPLIT])
    weight_here, wanted = together((weight_here, wanted))
    kinds = [list(range(kind, shards, 2)) for kind in range(2)]
    own = lax.all_gather(weight_here, "stretch", axis=0, tiled=True, axis_index_groups=kinds)
    picks = lax.all_to_all(wanted, "stretch", split_axis=0, concat_axis=0, tiled=True)
    picks, core = together((picks, core))
    rows = picked(0, picks)
    fetched = exchanged(rows)
    rows = picked(1, after(picks, rows))

    hidden_near, far, rows, picks, fetched = together((hidden_near, far, rows, picks, fetched))
    far = ahead(far)
    local0 = gradient(0, fetched)
    fetched = exchanged(rows)
    rows = picked(2, picks)

    here, gain, grads_soon, far, rows, picks, fetched, local0 = together(
        (here, gain, grads_soon, far, rows, picks, fetched, local0)
    )
    far, grads, part0 = ahead(far), back(here[1][GRAD_SPLIT:]), back(local0)
    local1 = gradient(1, fetched)
    fetched = exchanged(rows)
    rows = picked(3, picks)
    part1 = back(local1)

    rows, fetched, own, grads, far, part0, part1 = together(
        (rows, fetched, own, grads, far, part0, part1)
    )
    held = fetched
    local2 = query_gradient(owners, held, queries[0], grad_heads[0], 8 * HEAD_DIM, 4)
    fetched = exchanged(rows)
    part2 = back(local2)
    local3 = query_gradient(
        owners, after(held, local2), queries[0], grad_heads[0], 12 * HEAD_DIM, 4, 4 * HEAD_DIM
    )
    part3 = back(local3)
    other = lax.ppermute(own, "stretch", [(place, place ^ 1) for place in range(shards)])

    local3, part2, fetched = together((local3, part2, fetched))
    part4 = back(gradient(3, fetched))
    return finished(
        (part0, part1, part2, part3, part4),
        (hidden_near, far),
        (grads_soon, grads),
        own,
        other,
        core,
        gain,
    )[None]


def solution(mesh):
    in_specs = (
        P("section", "stretch", None),
        P("section", None),
        P("section", "stretch", None),
        P("section", "stretch", None, None),
        P("stretch", None),
        P("stretch", None),
        P("section", "stretch", None),
        P("section", "stretch", None),
        P("section", "stretch", None),
    )
    out_specs = P("section", "stretch", None)
    return jax.shard_map(local, mesh=mesh, in_specs=in_specs, out_specs=out_specs, check_vma=False)
```

```python
import functools

import jax
import jax.numpy as jnp
from jax import lax
from jax.experimental import pallas as pl
from jax.experimental.pallas import tpu as pltpu
from jax.sharding import PartitionSpec as P

HEAD_DIM = 128
STRETCH = 64
norm_eps = 1e-05
CHUNKS = ((0, 2), (4, 4), (8, 8), (2, 2))
HIDDEN_SPLIT = 240
GRAD_SPLIT = 352
PARTS = ((0, 2), (4, 4), (8, 4), (12, 4), (2, 2))
COLUMNS = 1024
VMEM = 60 << 20
SHARD = 128
STEP = 2


def passed_along(value, axis, steps):
    count = lax.axis_size(axis)
    pairs = [(source, (source + steps) % count) for source in range(count)]
    return lax.ppermute(value, axis, pairs)


def after(value, *before):
    return lax.optimization_barrier((value, *before))[0] if before else value


def pick_kernel(key_at, value_at, width, picks, table, out, rows, arrived, left):
    groups = arrived.shape[0]
    per = rows.shape[0] // groups
    for place in range(rows.shape[0]):
        row = picks[place]
        for start, at in ((key_at, 0), (value_at, width)):
            pltpu.make_async_copy(
                table.at[row, :, pl.ds(start, width)],
                rows.at[place, :, pl.ds(at, width)],
                arrived.at[place // per],
            ).start()
    moves = []
    for group in range(groups):
        slab = pl.ds(group * per, per)
        pltpu.make_async_copy(rows.at[slab], rows.at[slab], arrived.at[group]).wait()
        moves.append(pltpu.make_async_copy(rows.at[slab], out.at[slab], left.at[group]))
        moves[-1].start()
    for move in moves:
        move.wait()


def picked_rows(picks, table, first, width, qwidth):
    places = picks.shape[0]
    span = table.shape[1]
    size = places * span * 2 * width
    groups = 4
    return pl.pallas_call(
        functools.partial(pick_kernel, first, qwidth + first, width),
        out_shape=jax.ShapeDtypeStruct((places, span, 2 * width), table.dtype),
        grid_spec=pltpu.PrefetchScalarGridSpec(
            num_scalar_prefetch=1,
            grid=(1,),
            in_specs=[pl.BlockSpec(memory_space=pl.ANY)],
            out_specs=pl.BlockSpec(memory_space=pl.ANY),
            scratch_shapes=[
                pltpu.VMEM((places, span, 2 * width), table.dtype),
                pltpu.SemaphoreType.DMA((groups,)),
                pltpu.SemaphoreType.DMA((groups,)),
            ],
        ),
        compiler_params=pltpu.CompilerParams(vmem_limit_bytes=VMEM),
        cost_estimate=pl.CostEstimate(flops=0, transcendentals=0, bytes_accessed=4 * size),
        name="pick_rows",
    )(picks, table)


def side_by_side(block, left):
    right = left + HEAD_DIM
    zeros = jnp.zeros((STRETCH, HEAD_DIM), block.dtype)
    above = jnp.concatenate([block[:, left:right], zeros], axis=1)
    below = jnp.concatenate([zeros, block[:, right : right + HEAD_DIM]], axis=1)
    return jnp.concatenate([above, below], axis=0)


def attention_kernel(heads, owners, *refs):
    *rows, query, grad, out = refs
    for stretch in range(query.shape[0] // STRETCH):
        at = pl.ds(stretch * STRETCH, STRETCH)
        one_stretch(heads, *rows[4 * stretch : 4 * stretch + 4], query.at[at], grad.at[at], out.at[at])


def one_stretch(heads, first_keys, first_values, second_keys, second_values, query, grad, out):
    factor = HEAD_DIM ** (-0.5)
    width = heads * HEAD_DIM
    across = (((1,), (1,)), ((), ()))
    down = (((0,), (0,)), ((), ()))
    for left in range(0, width, 2 * HEAD_DIM):
        cols = slice(left, left + 2 * HEAD_DIM)
        keys = jnp.concatenate([first_keys[0, :, cols], second_keys[0, :, cols]], axis=0)
        values = jnp.concatenate([first_values[0, :, cols], second_values[0, :, cols]], axis=0)
        scores = lax.dot_general(
            keys, side_by_side(query, left), across, preferred_element_type=jnp.float32
        )
        dprob = lax.dot_general(
            values, side_by_side(grad, left), across, preferred_element_type=jnp.float32
        )
        exp_scores = jnp.exp((scores - jnp.max(scores, axis=0, keepdims=True)) * factor)
        share = 1.0 / jnp.sum(exp_scores, axis=0, keepdims=True)
        inner = jnp.sum(exp_scores * dprob, axis=0, keepdims=True) * share
        dscore = (exp_scores * (dprob - inner) * (share * factor)).astype(jnp.bfloat16)
        both = lax.dot_general(dscore, keys, down, preferred_element_type=jnp.float32)
        out[:, left : left + HEAD_DIM] = both[:STRETCH, :HEAD_DIM].astype(jnp.bfloat16)
        out[:, left + HEAD_DIM : left + 2 * HEAD_DIM] = both[STRETCH:, HEAD_DIM:].astype(
            jnp.bfloat16
        )


def query_gradient(owners, fetched, queries, grads, first, heads, skipped=0):
    width = heads * HEAD_DIM
    tokens = queries.shape[0]
    stretches = tokens // STRETCH
    span = fetched.shape[1]
    block = first // width
    rows = 2 * STEP

    within = fetched.shape[2] // (2 * width)

    def fetched_row(place, kind):
        return pl.BlockSpec(
            (1, span, width),
            lambda c, own: (own[rows * c + place], 0, kind * within + skipped // width),
        )

    tokens_step = STEP * STRETCH
    return pl.pallas_call(
        functools.partial(attention_kernel, heads),
        out_shape=jax.ShapeDtypeStruct((tokens, width), jnp.bfloat16),
        grid_spec=pltpu.PrefetchScalarGridSpec(
            num_scalar_prefetch=1,
            grid=(stretches // STEP,),
            in_specs=[fetched_row(place, kind) for place in range(rows) for kind in range(2)]
            + [
                pl.BlockSpec((tokens_step, width), lambda c, own: (c, block)),
                pl.BlockSpec((tokens_step, width), lambda c, own: (c, block)),
            ],
            out_specs=pl.BlockSpec((tokens_step, width), lambda c, own: (c, 0)),
        ),
        compiler_params=pltpu.CompilerParams(vmem_limit_bytes=VMEM),
        cost_estimate=pl.CostEstimate(
            flops=6 * tokens * STRETCH * width,
            transcendentals=tokens * STRETCH * heads,
            bytes_accessed=2 * (3 * tokens * width + 2 * stretches * span * 2 * width),
        ),
        name="query_gradient",
    )(owners, *([fetched] * (2 * rows)), queries, grads)


def stacked(refs):
    start = 0
    for ref in refs:
        yield ref, slice(start, start + ref.shape[0])
        start += ref.shape[0]


def finish_kernel(widths, counts, blocks, core, *refs):
    refs = list(refs)
    parts, hiddens, grads = ([refs.pop(0) for _ in range(count)] for count in counts)
    own, other, gain, out, scaled, dots, squares, whole = refs
    phase, block = pl.program_id(0), pl.program_id(1)
    model = blocks * COLUMNS

    @pl.when((phase == 0) & (block == 0))
    def _():
        for part, (first, width) in zip(parts, widths):
            whole[:, first : first + width] = part[...]

    @pl.when(phase == 0)
    def _():
        totals = []
        for weight in (own, other):
            totals.append(
                lax.dot_general(
                    whole[...],
                    weight[...],
                    (((1,), (1,)), ((), ())),
                    preferred_element_type=jnp.float32,
                )
            )
        ahead = core[0] == 0
        even = jnp.where(ahead, totals[0], totals[1])
        odd = jnp.where(ahead, totals[1], totals[0])
        tiles = []
        for lane in range(0, COLUMNS // 2, SHARD):
            tiles += [even[:, lane : lane + SHARD], odd[:, lane : lane + SHARD]]
        total = jnp.concatenate(tiles, axis=1)
        grad = total * gain[...]
        scaled[block] = grad
        for ref, rows in stacked(hiddens):
            values = ref[...].astype(jnp.float32)
            cross = grad[rows] * values
            square = values * values
            dot = cross[:, :128]
            norm = square[:, :128]
            for lane in range(128, COLUMNS, 128):
                dot = dot + cross[:, lane : lane + 128]
                norm = norm + square[:, lane : lane + 128]
            at = rows

            @pl.when(block == 0)
            def _():
                dots[at, :] = dot
                squares[at, :] = norm

            @pl.when(block > 0)
            def _():
                dots[at, :] += dot
                squares[at, :] += norm

    @pl.when((phase == 1) & (block == 0))
    def _():
        inv = lax.rsqrt(jnp.sum(squares[...], axis=-1, keepdims=True) / model + norm_eps)
        mean = inv * jnp.sum(dots[...], axis=-1, keepdims=True) / model
        squares[...] = jnp.broadcast_to(inv, squares.shape)
        dots[...] = jnp.broadcast_to(inv * inv * mean, dots.shape)

    @pl.when(phase == 1)
    def _():
        grad = scaled.at[block]
        across = COLUMNS // 128
        for values, rows in stacked(hiddens):
            for added, others in stacked(grads):
                start, stop = max(rows.start, others.start), min(rows.stop, others.stop)
                if start < stop:
                    at = slice(start, stop)
                    held = values[start - rows.start : stop - rows.start]
                    sent = added[start - others.start : stop - others.start]
                    inv = jnp.concatenate([squares[at, :]] * across, axis=1)
                    pull = jnp.concatenate([dots[at, :]] * across, axis=1)
                    out[at, :] = (
                        sent.astype(jnp.float32)
                        + inv * grad[at]
                        - pull * held.astype(jnp.float32)
                    ).astype(out.dtype)


def finished(parts, hiddens, grads, own, other, core, gain):
    tokens = sum(piece.shape[0] for piece in grads)
    model = gain.shape[1]
    widths = tuple((first * HEAD_DIM, heads * HEAD_DIM) for first, heads in PARTS)
    blocks = model // COLUMNS
    qwidth = own.shape[1]

    def early(phase, block):
        return jnp.where(phase == 0, block, blocks - 1)

    def late(phase, block):
        return jnp.where(phase == 0, 0, block)

    whole = [pl.BlockSpec((tokens, width), lambda p, b, c: (0, 0)) for _, width in widths]
    return pl.pallas_call(
        functools.partial(finish_kernel, widths, tuple(map(len, (parts, hiddens, grads))), blocks),
        out_shape=jax.ShapeDtypeStruct((tokens, model), jnp.bfloat16),
        grid_spec=pltpu.PrefetchScalarGridSpec(
            num_scalar_prefetch=1,
            grid=(2, blocks),
            in_specs=whole
            + [pl.BlockSpec((piece.shape[0], COLUMNS), lambda p, b, c: (0, b)) for piece in hiddens]
            + [
                pl.BlockSpec((piece.shape[0], COLUMNS), lambda p, b, c: (0, late(p, b)))
                for piece in grads
            ]
            + [pl.BlockSpec((COLUMNS // 2, qwidth), lambda p, b, c: (early(p, b), 0))] * 2
            + [pl.BlockSpec((1, COLUMNS), lambda p, b, c: (0, early(p, b)))],
            out_specs=pl.BlockSpec((tokens, COLUMNS), lambda p, b, c: (0, late(p, b))),
            scratch_shapes=[
                pltpu.VMEM((blocks, tokens, COLUMNS), jnp.float32),
                pltpu.VMEM((tokens, 128), jnp.float32),
                pltpu.VMEM((tokens, 128), jnp.float32),
                pltpu.VMEM((tokens, qwidth), jnp.bfloat16),
            ],
        ),
        compiler_params=pltpu.CompilerParams(vmem_limit_bytes=VMEM),
        cost_estimate=pl.CostEstimate(
            flops=2 * tokens * model * qwidth,
            transcendentals=0,
            bytes_accessed=2 * (model * qwidth + 4 * tokens * model),
        ),
        name="finish",
    )(core, *parts, *hiddens, *grads, own, other, gain)


def local(
    hidden, norm_gain, queries, cache, nbr_shard, nbr_slot, grad_heads, grad_out, query_weight
):
    shards = lax.axis_size("stretch")
    qwidth = queries.shape[2]
    together = lax.optimization_barrier

    def back(value):
        return passed_along(value, "section", -1)

    def ahead(value):
        return passed_along(value, "section", 1)

    def picked(chunk, picks):
        first_head, heads = CHUNKS[chunk]
        return picked_rows(picks, cache[0], first_head * HEAD_DIM, heads * HEAD_DIM, qwidth)

    def exchanged(rows):
        return lax.all_to_all(rows, "stretch", split_axis=0, concat_axis=0, tiled=True)

    def gradient(chunk, fetched):
        first_head, heads = CHUNKS[chunk]
        return query_gradient(
            owners, fetched, queries[0], grad_heads[0], first_head * HEAD_DIM, heads
        )

    here = hidden[0], grad_out[0]
    near = HIDDEN_SPLIT
    owners = nbr_shard.reshape(-1)
    asked = owners[:, None] == jnp.arange(shards)[None, :]
    wanted = jnp.sum(jnp.where(asked, nbr_slot.reshape(-1)[:, None], 0), axis=0)
    core = lax.rem(lax.axis_index("stretch"), 2).reshape(1)

    gain, weight_here = back(norm_gain), back(query_weight[0])
    hidden_near, far = back(here[0][:near]), ahead(here[0][near:])
    grads_soon = back(here[1][:GRAD_SPLIT])
    weight_here, wanted = together((weight_here, wanted))
    kinds = [list(range(kind, shards, 2)) for kind in range(2)]
    own = lax.all_gather(weight_here, "stretch", axis=0, tiled=True, axis_index_groups=kinds)
    picks = lax.all_to_all(wanted, "stretch", split_axis=0, concat_axis=0, tiled=True)
    picks, core = together((picks, core))
    rows = picked(0, picks)
    fetched = exchanged(rows)
    rows = picked(1, after(picks, rows))

    hidden_near, far, rows, picks, fetched = together((hidden_near, far, rows, picks, fetched))
    far = ahead(far)
    local0 = gradient(0, fetched)
    fetched = exchanged(rows)
    rows = picked(2, picks)

    here, gain, grads_soon, far, rows, picks, fetched, local0 = together(
        (here, gain, grads_soon, far, rows, picks, fetched, local0)
    )
    far, grads, part0 = ahead(far), back(here[1][GRAD_SPLIT:]), back(local0)
    local1 = gradient(1, fetched)
    fetched = exchanged(rows)
    rows = picked(3, picks)
    part1 = back(local1)

    rows, fetched, own, grads, far, part0, part1 = together(
        (rows, fetched, own, grads, far, part0, part1)
    )
    held = fetched
    local2 = query_gradient(owners, held, queries[0], grad_heads[0], 8 * HEAD_DIM, 4)
    fetched = exchanged(after(rows, local2))
    part2 = back(local2)
    local3 = query_gradient(
        owners, after(held, local2), queries[0], grad_heads[0], 12 * HEAD_DIM, 4, 4 * HEAD_DIM
    )
    part3 = back(local3)
    other = lax.ppermute(own, "stretch", [(place, place ^ 1) for place in range(shards)])

    local3, part2, fetched = together((local3, part2, fetched))
    part4 = back(gradient(3, fetched))
    return finished(
        (part0, part1, part2, part3, part4),
        (hidden_near, far),
        (grads_soon, grads),
        own,
        other,
        core,
        gain,
    )[None]


def solution(mesh):
    in_specs = (
        P("section", "stretch", None),
        P("section", None),
        P("section", "stretch", None),
        P("section", "stretch", None, None),
        P("stretch", None),
        P("stretch", None),
        P("section", "stretch", None),
        P("section", "stretch", None),
        P("section", "stretch", None),
    )
    out_specs = P("section", "stretch", None)
    return jax.shard_map(local, mesh=mesh, in_specs=in_specs, out_specs=out_specs, check_vma=False)
```
